32 devices in a mesh: grp: 2 (over x), head: 4 (over z), seq: 4 (over y, core).
Axes of the slice: x: 2, y: 2, z: 4, core: 2. Of those that a mesh axis runs over, the one named last changes fastest.
Arguments:
- queries: bfloat16 [64, 512, 128], P('head', 'seq'), may hold values from -6 to 6
- keys: bfloat16 [4, 512, 128], P('head', 'seq'), may hold values from -6 to 6
- values: bfloat16 [4, 512, 128], P('head', 'seq'), may hold values from -6 to 6
- feature_map: bfloat16 [64, 128, 128], P('head'), may hold values from -0.5 to 0.5
Outputs:
- feature_grad: float32 [64, 128, 128], P('head', ('grp', 'seq'))
The draws below stay inside these ranges and needn't reach their ends.
All inputs are finite; a program needn't handle non-finite values.
Results may differ from the reference program's by a relative error of at most 0.0044.
Values may be sent and summed in bfloat16 or wider, within the bound.
No kernel may reach another device: no remote copies, remote signals or barrier semaphores. Data moves between devices by JAX's collectives and lax.ppermute only.
A program may use at most 128 MiB of HBM per device.

```python
import jax
import jax.numpy as jnp
from jax import lax

DH = 128
GROUP = 16
FEAT = 128
KVH = 4
HEADS = 64
TOKENS = 512


def level_of(key, shape, shards, least, largest):
    def one(position, shards_of):
        steps = jax.random.uniform(jax.random.fold_in(jax.random.fold_in(key, 6), position), (shards_of,), jnp.float32, least / len(shards), largest / len(shards))
        return jnp.repeat(jnp.exp(steps), shape[position] // shards_of).reshape((-1,) + (1,) * (len(shape) - position - 1))

    loudness = one(*shards[0])
    for cut in shards[1:]:
        loudness = loudness * one(*cut)
    return loudness


def normal_values(key, dims, deviation, bound, cuts=(), kind=jnp.bfloat16):
    factor_of = level_of(key, dims, cuts, -0.22, 0.18) if cuts else 1.0
    drawn = jax.random.normal(key, dims, jnp.float32) * deviation * factor_of
    return jnp.minimum(jnp.maximum(drawn, -bound), bound).astype(kind)


def setup_inputs(seed: int = 0) -> dict:
    key_list = jax.random.split(jax.random.key(seed), 5)
    return {
        "queries": normal_values(key_list[0], (HEADS, TOKENS, DH), 1.0, 6.0, ((0, 4), (1, 4))),
        "keys": normal_values(key_list[1], (KVH, TOKENS, DH), 1.0, 6.0, ((0, 4), (1, 4))),
        "values": normal_values(key_list[2], (KVH, TOKENS, DH), 1.0, 6.0, ((0, 4), (1, 4))),
        "feature_map": normal_values(key_list[3], (HEADS, DH, FEAT), DH ** -0.5, 0.5, ((0, 4),)),
    }


def teacher_head(queries, keys, values, index):
    kv_index = index // GROUP
    query_rows = queries[index]
    key_rows = keys[kv_index]
    value_rows = values[kv_index]
    scores = jnp.dot(query_rows, key_rows.T, preferred_element_type=jnp.float32) / jnp.sqrt(jnp.float32(DH))
    causal = jnp.tril(jnp.ones((TOKENS, TOKENS), dtype=bool))
    weights = jnp.where(causal, jnp.exp(scores), jnp.float32(0.0))
    denom = lax.optimization_barrier(jnp.sum(weights, axis=1))
    numer = jnp.dot(weights.astype(jnp.bfloat16), value_rows, preferred_element_type=jnp.float32)
    return (numer / denom[:, None]).astype(jnp.bfloat16)

def student_head(query_rows, key_rows, value_rows, wmat):
    hp = lax.Precision.HIGHEST
    phi_q = jnp.exp(jnp.dot(query_rows, wmat, precision=hp))
    phi_k = jnp.exp(jnp.dot(key_rows, wmat, precision=hp))
    causal = jnp.tril(jnp.ones((TOKENS, TOKENS), dtype=jnp.float32))
    scores = jnp.dot(phi_q, phi_k.T, precision=hp) * causal
    numer = jnp.dot(scores, value_rows, precision=hp)
    denom = lax.optimization_barrier(jnp.sum(scores, axis=1))
    return numer / denom[:, None]

def reference(queries, keys, values, feature_map):
    indices = jnp.arange(HEADS, dtype=jnp.int32)
    teacher = lax.map(lambda idx: teacher_head(queries, keys, values, idx), indices)
    target = teacher.astype(jnp.float32)
    query_f = queries.astype(jnp.float32)
    key_f = keys.astype(jnp.float32)
    value_f = values.astype(jnp.float32)

    def loss_of(weights):

        def one_head(index):
            kv_index = index // GROUP
            student = student_head(query_f[index], key_f[kv_index], value_f[kv_index], weights[index])
            return jnp.sum((student - target[index]) ** 2)
        return jnp.sum(lax.map(one_head, indices)) / jnp.float32(TOKENS)
    return jax.grad(loss_of)(feature_map.astype(jnp.float32))
```

```python
import functools

import jax
import jax.numpy as jnp
from jax import lax
from jax.experimental import pallas as pl
from jax.experimental.pallas import tpu as pltpu
from jax.sharding import PartitionSpec as P

F32 = jnp.float32
BF16 = jnp.bfloat16
NN = (((1,), (0,)), ((), ()))
NT = (((1,), (1,)), ((), ()))
TN = (((0,), (0,)), ((), ()))


def mm(a, b, dims=NN):
    return lax.dot_general(a, b, dims, preferred_element_type=F32)


def split(x):
    high = x.astype(BF16)
    return high, (x - high.astype(F32)).astype(BF16)


def cat(parts, axis):
    return jnp.concatenate(parts, axis)


def body(total, place, q_own, q_pair, w_ref, kv_own, kv_pair, hop_own, hop_pair, out, step):
    tokens, dh = q_own.shape[-2:]
    rows = 2 * tokens
    core, chip = place[0], place[1]
    scale = 1.0 / (dh**0.5)
    ones = jnp.ones((rows, dh), BF16)

    def position(axis):
        index = lax.broadcasted_iota(jnp.int32, (rows, rows), axis)
        return jnp.where((index < tokens) == (core == 0), index % tokens, tokens + index % tokens)

    seen = position(1) <= position(0)
    key = cat([kv_own[0], kv_pair[0]], 0)
    value = cat([cat([kv_own[1], kv_pair[1]], 0), ones], 1)
    hops = hop_own.shape[0]

    def head(h):
        query = cat([q_own[h], q_pair[h]], 0)
        wmat = w_ref[h]
        phi_q = jnp.exp(mm(query, wmat))
        phi_k = jnp.exp(mm(key, wmat))
        qh, ql = split(phi_q)
        kh, kl = split(phi_k)
        p = jnp.where(seen, jnp.exp(mm(query, key, NT) * scale), 0.0)
        denom_t = jnp.sum(p, axis=1, keepdims=True)
        numer_t = mm(p.astype(BF16), value[:, :dh])
        a = jnp.where(seen, mm(cat([qh, ql, qh], 1), cat([kh, kh, kl], 1), NT), 0.0)
        ah, al = split(a)
        both = mm(cat([ah, al], 1), cat([value, value], 0))

        def earlier(hop, carry):
            state, numer_t, denom_t = carry
            live = hop < chip
            key_j = cat([hop_own[hop, 0], hop_pair[hop, 0]], 0)
            value_j = cat([cat([hop_own[hop, 1], hop_pair[hop, 1]], 0), ones], 1)
            p = jnp.where(live, jnp.exp(mm(query, key_j, NT) * scale), 0.0)
            denom_t = denom_t + jnp.sum(p, axis=1, keepdims=True)
            numer_t = numer_t + mm(p.astype(BF16), value_j[:, :dh])
            phi_j = jnp.where(live, jnp.exp(mm(key_j, wmat)), 0.0)
            jh, jl = split(phi_j)
            state = state + mm(cat([jh, jl], 0), cat([value_j, value_j], 0), TN)
            return state, numer_t, denom_t

        carry = (jnp.zeros((wmat.shape[1], 2 * dh), F32), numer_t, denom_t)
        if hops == 1:
            carry = earlier(0, carry)
        else:
            carry = lax.fori_loop(0, hops, earlier, carry)
        state, numer_t, denom_t = carry
        sh, sl = split(state)
        both = both + mm(cat([qh, ql, qh], 1), cat([sh, sh, sl], 0))
        target = (numer_t / denom_t).astype(BF16).astype(F32)
        inverse = 1.0 / both[:, dh:]
        student = both[:, :dh] * inverse
        cotangent = (student - target) * (2.0 / total) * inverse
        g = cat([cotangent, -cotangent * student], 1)
        gh, gl = split(g)
        da = jnp.where(seen, mm(cat([gh, gl], 1), cat([value, value], 1), NT), 0.0)
        dah, dal = split(da)
        wide_k = mm(dah, cat([kh, kl], 1))
        dphi_q = wide_k[:, :dh] + wide_k[:, dh:] + mm(dal, kh)
        dphi_q = dphi_q + mm(cat([gh, gl, gh], 1), cat([sh, sh, sl], 1), NT)
        wide_q = mm(dah, cat([qh, ql], 1), TN)
        dphi_k = wide_q[:, :dh] + wide_q[:, dh:] + mm(dal, qh, TN)
        zqh, zql = split(dphi_q * phi_q)
        zkh, zkl = split(dphi_k * phi_k)
        wide = mm(cat([query, key], 0), cat([cat([zqh, zql], 1), cat([zkh, zkl], 1)], 0), TN)
        grad = wide[:, : wmat.shape[1]] + wide[:, wmat.shape[1] :]
        ds = mm(cat([qh, qh, ql], 0), cat([gh, gl, gh], 0), TN)
        dsh, dsl = split(ds)

        def back(hop, grad):
            live = hop < chip
            key_j = cat([hop_own[hop, 0], hop_pair[hop, 0]], 0)
            value_j = cat([cat([hop_own[hop, 1], hop_pair[hop, 1]], 0), ones], 1)
            phi_j = jnp.where(live, jnp.exp(mm(key_j, wmat)), 0.0)
            dphi_j = mm(cat([value_j, value_j], 1), cat([dsh, dsl], 1), NT)
            zh, zl = split(dphi_j * phi_j)
            wide = mm(key_j, cat([zh, zl], 1), TN)
            return grad + wide[:, : wmat.shape[1]] + wide[:, wmat.shape[1] :]

        if hops == 1:
            grad = back(0, grad)
        else:
            grad = lax.fori_loop(0, hops, back, grad)
        out[h] = grad

    heads = w_ref.shape[0]

    def group(i, _):
        for j in range(step):
            head(i * step + j)
        return 0

    lax.fori_loop(0, heads // step, group, 0)


def gradients(place, q_own, q_pair, wmat, kv_own, kv_pair, hop_own, hop_pair, total, step=2):
    vmem = pl.BlockSpec(memory_space=pltpu.VMEM)
    return pl.pallas_call(
        lambda *refs: body(total, *refs, step),
        in_specs=[pl.BlockSpec(memory_space=pltpu.SMEM)] + [vmem] * 7,
        out_specs=vmem,
        out_shape=jax.ShapeDtypeStruct(wmat.shape, F32),
        name="gradients",
    )(place, q_own, q_pair, wmat, kv_own, kv_pair, hop_own, hop_pair)


def per_device(queries, keys, values, feature_map):
    count = lax.axis_size("seq")
    groups = lax.axis_size("grp")
    chips = count // 2
    seq = lax.axis_index("seq")
    core, chip = seq % 2, seq // 2
    total = keys.shape[1] * count
    heads = queries.shape[0] // 2
    kv = cat([keys, values], 0)
    swap = [(i, i ^ 1) for i in range(count)]
    hop_own = jnp.stack(
        [
            lax.ppermute(kv, "seq", [(i, i + 2 * k) for i in range(count - 2 * k)])
            for k in range(1, chips)
        ]
    )
    halves = queries.reshape(2, heads, *queries.shape[1:])
    q_own = lax.dynamic_index_in_dim(halves, core, 0, False)
    q_pair = lax.ppermute(lax.dynamic_index_in_dim(halves, 1 - core, 0, False), "seq", swap)
    kv_pair = lax.ppermute(kv, "seq", swap)
    hop_pair = lax.ppermute(hop_own, "seq", swap)
    wmat = lax.dynamic_slice_in_dim(feature_map, core * heads, heads, 0)
    place = jnp.stack([core, chip]).astype(jnp.int32)
    grad = gradients(place, q_own, q_pair, wmat, kv, kv_pair, hop_own, hop_pair, total)
    mine = wmat.shape[1] // groups
    grad = lax.dynamic_slice_in_dim(grad, lax.axis_index("grp") * mine, mine, 1)
    grad = grad.reshape(heads, chips, 2, mine // count, grad.shape[-1])
    away = lax.ppermute(lax.dynamic_index_in_dim(grad, 1 - core, 2, False), "seq", swap)
    stay = lax.dynamic_index_in_dim(grad, core, 2, False)
    first = core == 0
    part = cat([jnp.where(first, stay, away), jnp.where(first, away, stay)], 0)
    result = lax.dynamic_index_in_dim(part, chip, 1, False)
    for k in range(1, chips):
        send = lax.dynamic_index_in_dim(part, (chip + k) % chips, 1, False)
        ring = [(i, (i + 2 * k) % count) for i in range(count)]
        result = result + lax.ppermute(send, "seq", ring)
    return result


def solution(mesh):
    return jax.shard_map(
        per_device,
        mesh=mesh,
        in_specs=(
            P("head", "seq", None),
            P("head", "seq", None),
            P("head", "seq", None),
            P("head", None, None),
        ),
        out_specs=P("head", ("grp", "seq"), None),
        check_vma=False,
    )
```

```python
import jax
import jax.numpy as jnp
from jax import lax
from jax.experimental import pallas as pl
from jax.experimental.pallas import tpu as pltpu
from jax.sharding import PartitionSpec as P

F32 = jnp.float32
BF16 = jnp.bfloat16
WIRE = BF16
NN = (((1,), (0,)), ((), ()))
NT = (((1,), (1,)), ((), ()))
TN = (((0,), (0,)), ((), ()))


def mm(a, b, dims=NN):
    return lax.dot_general(a, b, dims, preferred_element_type=F32)


def split(x):
    high = x.astype(BF16)
    return high, (x - high.astype(F32)).astype(BF16)


def cat(parts, axis):
    return jnp.concatenate(parts, axis)


def interleave(make, heads, step):
    def group(i, _):
        running = [make(i * step + j) for j in range(step)]
        while running:
            running = [r for r in running if next(r, True) is None]
        return 0

    lax.fori_loop(0, heads // step, group, 0)


def extended(value):
    return cat([value, jnp.ones(value.shape, BF16)], 1)


def own_block(core, kv_own, kv_pair):
    tokens = kv_own.shape[1]
    rows = 2 * tokens

    def position(axis):
        index = lax.broadcasted_iota(jnp.int32, (rows, rows), axis)
        return jnp.where((index < tokens) == (core == 0), index % tokens, tokens + index % tokens)

    key = cat([kv_own[0], kv_pair[0]], 0)
    value = extended(cat([kv_own[1], kv_pair[1]], 0))
    return position(1) <= position(0), key, value


def cotangents(total, numer_t, denom_t, both):
    dh = numer_t.shape[1]
    target = (numer_t / denom_t).astype(BF16).astype(F32)
    inverse = 1.0 / both[:, dh:]
    student = both[:, :dh] * inverse
    g = ((student - target) * (2.0 / total) * inverse).astype(BF16)
    return g, jnp.sum(g.astype(F32) * student, axis=1, keepdims=True)


def score_cotangent(seen, g, value, shift):
    return split(jnp.where(seen, mm(g, value[:, : g.shape[1]], NT) - shift, 0.0))


def map_gradient(query, key, dphi_q, phi_q, dphi_k, phi_k):
    zqh, zql = split(dphi_q * phi_q)
    zkh, zkl = split(dphi_k * phi_k)
    stacked = cat([cat([zqh, zql], 1), cat([zkh, zkl], 1)], 0)
    return mm(cat([query, key], 0), stacked, TN)


def first_body(step, place, q_own, q_pair, w_ref, kv_own, kv_pair, *outs):
    numer_ref, denom_ref, both_ref = outs
    dh = q_own.shape[-1]
    core = place[0]
    scale = 1.0 / (dh**0.5)
    seen, key, value = own_block(core, kv_own, kv_pair)
    heads = w_ref.shape[0]

    def forward(h):
        query = cat([q_own[h], q_pair[h]], 0)
        wmat = w_ref[h]
        phi_q = jnp.exp(mm(query, wmat))
        phi_k = jnp.exp(mm(key, wmat))
        qh, kh = phi_q.astype(BF16), phi_k.astype(BF16)
        yield
        p = jnp.where(seen, jnp.exp(mm(query, key, NT) * scale), 0.0)
        a = jnp.where(seen, mm(qh, kh, NT), 0.0)
        yield
        denom_ref[h] = jnp.sum(p, axis=1, keepdims=True)
        numer_ref[h] = mm(p.astype(BF16), value[:, :dh])
        both_ref[h] = mm(cat(split(a), 1), cat([value, value], 0))

    interleave(forward, heads, step)


def second_body(total, step, place, q_own, q_pair, w_ref, kv_own, kv_pair, *refs):
    numer_ref, denom_ref, both_ref, hop_own, hop_pair, grad_ref = refs
    dh = q_own.shape[-1]
    core, chip = place[0], place[1]
    scale = 1.0 / (dh**0.5)
    hops = hop_own.shape[0]
    heads, _, feats = w_ref.shape

    def hop_block(hop):
        key_j = cat([hop_own[hop, 0], hop_pair[hop, 0]], 0)
        return key_j, extended(cat([hop_own[hop, 1], hop_pair[hop, 1]], 0))

    def loop(function, carry):
        return function(0, carry) if hops == 1 else lax.fori_loop(0, chip, function, carry)

    def whole(h):
        seen, key, value = own_block(core, kv_own, kv_pair)
        query = cat([q_own[h], q_pair[h]], 0)
        wmat = w_ref[h]

        def earlier(hop, carry):
            state, total_j, numer_t, denom_t = carry
            key_j, value_j = hop_block(hop)
            p = jnp.exp(mm(query, key_j, NT) * scale)
            denom_t = denom_t + jnp.sum(p, axis=1, keepdims=True)
            numer_t = numer_t + mm(p.astype(BF16), value_j[:, :dh])
            phi_j = jnp.exp(mm(key_j, wmat)).astype(BF16)
            state = state + mm(phi_j, value_j, TN)
            total_j = total_j + jnp.sum(phi_j.astype(F32), axis=0, keepdims=True)
            return state, total_j, numer_t, denom_t

        empty = (jnp.zeros((feats, 2 * dh), F32), jnp.zeros((1, feats), F32))
        state, total_j, numer_t, denom_t = loop(earlier, empty + (numer_ref[h], denom_ref[h]))
        phi_q, phi_k = jnp.exp(mm(query, wmat)), jnp.exp(mm(key, wmat))
        yield
        qh, kh = phi_q.astype(BF16), phi_k.astype(BF16)
        sh, sl = split(state)
        both = both_ref[h] + mm(cat([qh, qh], 1), cat([sh, sl], 0))
        yield
        g, shift = cotangents(total, numer_t, denom_t, both)
        yield
        da, dal = score_cotangent(seen, g, value, shift)
        yield
        dphi_q = mm(cat([da, dal], 1), cat([kh, kh], 0)) - shift * total_j
        dphi_q = dphi_q + mm(cat([g, g], 1), cat([sh[:, :dh], sl[:, :dh]], 1), NT)
        dphi_k = mm(cat([da, dal], 0), cat([qh, qh], 0), TN)
        dsh, dsl = split(mm(qh, g, TN))
        lost = jnp.sum(qh.astype(F32) * shift, axis=0, keepdims=True)
        yield
        wide = map_gradient(query, key, dphi_q, phi_q, dphi_k, phi_k)
        yield

        def back(hop, wide):
            key_j, value_j = hop_block(hop)
            value_j = value_j[:, :dh]
            phi_j = jnp.exp(mm(key_j, wmat))
            dphi_j = mm(cat([value_j, value_j], 1), cat([dsh, dsl], 1), NT) - lost
            zh, zl = split(dphi_j * phi_j)
            return wide + mm(key_j, cat([zh, zl], 1), TN)

        wide = loop(back, wide)
        yield
        grad_ref[h] = wide[:, :feats] + wide[:, feats:]

    @pl.when(chip != 0)
    def _():
        interleave(whole, heads, step)

    def alone(h):
        seen, key, value = own_block(core, kv_own, kv_pair)
        query = cat([q_own[h], q_pair[h]], 0)
        phi_q, phi_k = jnp.exp(mm(query, w_ref[h])), jnp.exp(mm(key, w_ref[h]))
        qh, kh = phi_q.astype(BF16), phi_k.astype(BF16)
        g, shift = cotangents(total, numer_ref[h], denom_ref[h], both_ref[h])
        yield
        da, dal = score_cotangent(seen, g, value, shift)
        yield
        dphi_q = mm(cat([da, dal], 1), cat([kh, kh], 0))
        dphi_k = mm(cat([da, dal], 0), cat([qh, qh], 0), TN)
        yield
        wide = map_gradient(query, key, dphi_q, phi_q, dphi_k, phi_k)
        yield
        grad_ref[h] = wide[:, :feats] + wide[:, feats:]

    @pl.when(chip == 0)
    def _():
        interleave(alone, heads, step)


def call(function, outs, *operands):
    vmem = pl.BlockSpec(memory_space=pltpu.VMEM)
    return pl.pallas_call(
        function,
        in_specs=[pl.BlockSpec(memory_space=pltpu.SMEM)] + [vmem] * (len(operands) - 1),
        out_specs=[vmem] * len(outs),
        out_shape=[jax.ShapeDtypeStruct(s, F32) for s in outs],
        compiler_params=pltpu.CompilerParams(vmem_limit_bytes=16 << 20),
        cost_estimate=pl.CostEstimate(flops=2 * 10**9, bytes_accessed=10**7, transcendentals=10**6),
    )(*operands)


def per_device(queries, keys, values, feature_map):
    count, groups = lax.axis_size("seq"), lax.axis_size("grp")
    chips = count // 2
    seq, grp = lax.axis_index("seq"), lax.axis_index("grp")
    core, chip = seq & 1, seq >> 1
    tokens, dh = keys.shape[1:]
    total = tokens * count
    feats = feature_map.shape[2]
    hn = queries.shape[0] // (2 * groups)
    lines = dh // (groups * count)
    step = hn if hn <= 4 else 1
    swap = [(i, i ^ 1) for i in range(count)]

    def mine(array, half):
        split_heads = array.reshape(2 * groups, hn, *array.shape[1:])
        return lax.dynamic_index_in_dim(split_heads, half * groups + grp, 0, False)

    kv = cat([keys, values], 0)
    hops = []
    for k in range(1, chips):
        ring = [(i, (i + 2 * k) % count) for i in range(count)]
        hops.append(lax.ppermute(kv, "seq", ring))
    place = jnp.stack([core, chip]).astype(jnp.int32)
    kv_pair = lax.ppermute(kv, "seq", swap)
    q_pair = lax.ppermute(mine(queries, 1 - core), "seq", swap)
    local = (place, mine(queries, core), q_pair, mine(feature_map, core), kv, kv_pair)
    rows = 2 * tokens
    state = [(hn, rows, dh), (hn, rows, 1), (hn, rows, 2 * dh)]
    state = call(lambda *r: first_body(step, *r), state, *local)
    hop_own = jnp.stack(hops)
    hop_pair = lax.ppermute(hop_own, "seq", swap)
    (grad,) = call(
        lambda *r: second_body(total, step, *r),
        [(hn, dh, feats)],
        *local,
        *state,
        hop_own,
        hop_pair,
    )
    peers = grad.reshape(hn, groups * count, lines, feats).transpose(1, 0, 2, 3)
    got = lax.all_to_all(peers.astype(WIRE), ("grp", "seq"), 0, 0, tiled=True)
    parts = got.reshape(groups, chips, 2, hn, lines, feats).astype(F32)
    return parts.sum(1).transpose(1, 0, 2, 3, 4).reshape(queries.shape[0], lines, feats)


def solution(mesh):
    return jax.shard_map(
        per_device,
        mesh=mesh,
        in_specs=(
            P("head", "seq", None),
            P("head", "seq", None),
            P("head", "seq", None),
            P("head", None, None),
        ),
        out_specs=P("head", ("grp", "seq"), None),
        check_vma=False,
    )
```

```python
import jax
import jax.numpy as jnp
from jax import lax
from jax.experimental import pallas as pl
from jax.experimental.pallas import tpu as pltpu
from jax.sharding import PartitionSpec as P

F32 = jnp.float32
BF16 = jnp.bfloat16
WIRE = BF16
NN = (((1,), (0,)), ((), ()))
NT = (((1,), (1,)), ((), ()))
TN = (((0,), (0,)), ((), ()))


def mm(a, b, dims=NN):
    return lax.dot_general(a, b, dims, preferred_element_type=F32)


def split(x):
    high = x.astype(BF16)
    return high, (x - high.astype(F32)).astype(BF16)


def cat(parts, axis):
    return jnp.concatenate(parts, axis)


def interleave(make, heads, step):
    def group(i, _):
        running = [make(i * step + j) for j in range(step)]
        while running:
            running = [r for r in running if next(r, True) is None]
        return 0

    lax.fori_loop(0, heads // step, group, 0)


def add_rows(x):
    return jnp.sum(x, axis=0, keepdims=True)


def own_block(core, kv_own, kv_pair):
    tokens = kv_own.shape[1]
    rows = 2 * tokens

    def position(axis):
        index = lax.broadcasted_iota(jnp.int32, (rows, rows), axis)
        return jnp.where((index < tokens) == (core == 0), index % tokens, tokens + index % tokens)

    key = cat([kv_own[0], kv_pair[0]], 0)
    value = cat([kv_own[1], kv_pair[1]], 0)
    return position(0) <= position(1), key, value


def features(wmat_t, query, key):
    return jnp.exp(mm(wmat_t, query, NT)), jnp.exp(mm(wmat_t, key, NT))


def first_body(step, place, q_own, q_pair, w_ref, kv_own, kv_pair, state_ref):
    dh = q_own.shape[-1]
    scale = 1.0 / (dh**0.5)
    seen, key, value = own_block(place[0], kv_own, kv_pair)
    value_t = value.T
    heads, _, _ = w_ref.shape

    def forward(h):
        query = cat([q_own[h], q_pair[h]], 0)
        wmat_t = w_ref[h].T
        phi_q, phi_k = features(wmat_t, query, key)
        yield
        p = jnp.where(seen, jnp.exp(mm(key, query, NT) * scale), 0.0)
        yield
        a = jnp.where(seen, mm(phi_k.astype(BF16), phi_q.astype(BF16), TN), 0.0)
        yield
        sums = cat([add_rows(p), add_rows(a), jnp.zeros((6, p.shape[1]), F32)], 0)
        state_ref[h, 2 * dh :] = sums
        state_ref[h, :dh] = mm(value_t, p.astype(BF16))
        yield
        state_ref[h, dh : 2 * dh] = mm(cat([value_t, value_t], 1), cat(split(a), 0))

    interleave(forward, heads, step)


def second_body(total, step, place, q_own, q_pair, w_ref, kv_own, kv_pair, state_ref, hop_own, hop_pair, grad_ref):
    dh = q_own.shape[-1]
    core, chip = place[0], place[1]
    scale = 1.0 / (dh**0.5)
    hops = hop_own.shape[0]
    heads, _, feats = w_ref.shape

    def hop_block(hop):
        key_j = cat([hop_own[hop, 0], hop_pair[hop, 0]], 0)
        return key_j, cat([hop_own[hop, 1], hop_pair[hop, 1]], 0)

    def cotangents(numer_t, denom_t, numer_s, denom_s):
        target = (numer_t * (1.0 / denom_t)).astype(BF16).astype(F32)
        inverse = 1.0 / denom_s
        student = numer_s * inverse
        g = ((student - target) * (inverse * (2.0 / total))).astype(BF16)
        return g, add_rows(g.astype(F32) * student)

    def score_back(seen, value, g, shift):
        return split(jnp.where(seen, mm(value, g) - shift, 0.0))

    def local_back(dah, dal, qh, kh):
        dphi_q = mm(cat([kh, kh], 1), cat([dah, dal], 0))
        return dphi_q, mm(cat([qh, qh], 1), cat([dah, dal], 1), NT)

    def stacked(dz):
        return cat(split(dz), 0)

    def saved(h):
        numer_t, numer_s = state_ref[h, :dh], state_ref[h, dh : 2 * dh]
        sums = state_ref[h, 2 * dh :]
        return numer_t, sums[0:1], numer_s, sums[1:2]

    def finish(h, wide):
        grad_ref[h] = (wide[:feats] + wide[feats:]).T

    def whole(h):
        seen, key, value = own_block(core, kv_own, kv_pair)
        query = cat([q_own[h], q_pair[h]], 0)
        wmat_t = w_ref[h].T

        def earlier(hop, carry):
            state, state_t, total_j, numer_t, denom_t = carry[:5]
            key_j, value_j = hop_block(hop)
            if pre is None:
                p = jnp.exp(mm(key_j, query, NT) * scale)
                phi_j = jnp.exp(mm(wmat_t, key_j, NT))
            else:
                p, phi_j = pre
            ph = phi_j.astype(BF16)
            value_jt = value_j.T
            denom_t = denom_t + add_rows(p)
            numer_t = numer_t + mm(value_jt, p.astype(BF16))
            state = state + mm(ph, value_j)
            state_t = state_t + mm(value_jt, ph, NT)
            total_j = total_j + jnp.sum(ph.astype(F32), axis=1, keepdims=True)
            sums = (state, state_t, total_j, numer_t, denom_t)
            return sums + (phi_j,) if hops == 1 else sums

        numer_t, denom_t, numer_s, denom_s = saved(h)
        phi_q, phi_k = features(wmat_t, query, key)
        qh, kh = phi_q.astype(BF16), phi_k.astype(BF16)
        square = jnp.zeros((feats, dh), F32), jnp.zeros((dh, feats), F32)
        carry = square + (jnp.zeros((feats, 1), F32), numer_t, denom_t)
        pre = None
        if hops == 1:
            key_j = hop_block(0)[0]
            phi_j = jnp.exp(mm(wmat_t, key_j, NT))
            yield
            pre = jnp.exp(mm(key_j, query, NT) * scale), phi_j
            yield
            carry = earlier(0, carry)
        else:
            carry = lax.fori_loop(0, chip, earlier, carry)
        state, state_t, total_j, numer_t, denom_t = carry[:5]
        yield
        numer_s = numer_s + mm(cat(split(state_t), 1), cat([qh, qh], 0))
        denom_s = denom_s + add_rows(qh.astype(F32) * total_j)
        yield
        g, shift = cotangents(numer_t, denom_t, numer_s, denom_s)
        yield
        dah, dal = score_back(seen, value, g, shift)
        ds = mm(qh, g, NT)
        yield
        dphi_q, dphi_k = local_back(dah, dal, qh, kh)
        yield
        lost = jnp.sum(qh.astype(F32) * shift, axis=1, keepdims=True)
        dphi_q = dphi_q + mm(cat(split(state), 1), cat([g, g], 0)) - total_j * shift
        yield
        dsw = cat(split(ds), 1)

        def step_back(value_j, phi_j):
            return stacked((mm(dsw, cat([value_j, value_j], 1), NT) - lost) * phi_j)

        if hops == 1:
            key_j, value_j = hop_block(0)
            dz_j = step_back(value_j, carry[5])
            yield
            dz_q = stacked(dphi_q * phi_q)
            dz_k = stacked(dphi_k * phi_k)
            yield
            wide = mm(cat([dz_q, dz_k, dz_j], 1), cat([query, key, key_j], 0))
        else:
            dz = cat([stacked(dphi_q * phi_q), stacked(dphi_k * phi_k)], 1)
            wide = mm(dz, cat([query, key], 0))

            def back(hop, wide):
                key_j, value_j = hop_block(hop)
                phi_j = jnp.exp(mm(wmat_t, key_j, NT))
                return wide + mm(step_back(value_j, phi_j), key_j)

            wide = lax.fori_loop(0, chip, back, wide)
        yield
        finish(h, wide)

    @pl.when(chip != 0)
    def _():
        interleave(whole, heads, step)

    def alone(h):
        seen, key, value = own_block(core, kv_own, kv_pair)
        query = cat([q_own[h], q_pair[h]], 0)
        wmat_t = w_ref[h].T
        numer_t, denom_t, numer_s, denom_s = saved(h)
        phi_q, phi_k = features(wmat_t, query, key)
        qh, kh = phi_q.astype(BF16), phi_k.astype(BF16)
        g, shift = cotangents(numer_t, denom_t, numer_s, denom_s)
        yield
        dah, dal = score_back(seen, value, g, shift)
        yield
        dphi_q, dphi_k = local_back(dah, dal, qh, kh)
        yield
        dz = cat([stacked(dphi_q * phi_q), stacked(dphi_k * phi_k)], 1)
        wide = mm(dz, cat([query, key], 0))
        yield
        finish(h, wide)

    @pl.when(chip == 0)
    def _():
        interleave(alone, heads, step)


def call(function, outs, *operands):
    vmem = pl.BlockSpec(memory_space=pltpu.VMEM)
    return pl.pallas_call(
        function,
        in_specs=[pl.BlockSpec(memory_space=pltpu.SMEM)] + [vmem] * (len(operands) - 1),
        out_specs=[vmem] * len(outs),
        out_shape=[jax.ShapeDtypeStruct(s, F32) for s in outs],
        compiler_params=pltpu.CompilerParams(vmem_limit_bytes=16 << 20),
        cost_estimate=pl.CostEstimate(flops=2 * 10**9, bytes_accessed=10**7, transcendentals=10**6),
    )(*operands)


def per_device(queries, keys, values, feature_map):
    count, groups = lax.axis_size("seq"), lax.axis_size("grp")
    chips = count // 2
    seq, grp = lax.axis_index("seq"), lax.axis_index("grp")
    core, chip = seq & 1, seq >> 1
    tokens, dh = keys.shape[1:]
    total = tokens * count
    feats = feature_map.shape[2]
    hn = queries.shape[0] // (2 * groups)
    lines = dh // (groups * count)
    step = hn if hn <= 4 else 1
    swap = [(i, i ^ 1) for i in range(count)]

    def mine(array, half):
        split_heads = array.reshape(2 * groups, hn, *array.shape[1:])
        return lax.dynamic_index_in_dim(split_heads, half * groups + grp, 0, False)

    kv = jnp.where(lax.broadcasted_iota(jnp.int32, (2, tokens, dh), 0) == 0, keys, values)
    hops = []
    for k in range(1, chips):
        ring = [(i, (i + 2 * k) % count) for i in range(count)]
        hops.append(lax.ppermute(kv, "seq", ring))
    place = jnp.stack([core, chip]).astype(jnp.int32)
    kv_pair = lax.ppermute(kv, "seq", swap)
    q_pair = lax.ppermute(mine(queries, 1 - core), "seq", swap)
    local = (place, mine(queries, core), q_pair, mine(feature_map, core), kv, kv_pair)
    rows = 2 * tokens
    state = [(hn, 2 * dh + 8, rows)]
    state = call(lambda *r: first_body(step, *r), state, *local)
    hop_own = jnp.stack(hops)
    hop_pair = lax.ppermute(hop_own, "seq", swap)
    (grad,) = call(
        lambda *r: second_body(total, step, *r),
        [(hn, dh, feats)],
        *local,
        *state,
        hop_own,
        hop_pair,
    )
    grad = grad.reshape(hn, groups, chips, 2, lines, feats)
    keep = lax.dynamic_index_in_dim(grad, core, 3, False)
    got = lax.ppermute(lax.dynamic_index_in_dim(grad, 1 - core, 3, False), "seq", swap)
    low = core == 0
    part = jnp.stack([jnp.where(low, keep, got), jnp.where(low, got, keep)])

    def rows_for(turn, ahead):
        there = lax.dynamic_index_in_dim(part, (grp + turn) % groups, 2, False)
        return lax.dynamic_index_in_dim(there, (chip + ahead) % chips, 2, False)

    received = [rows_for(0, 0)] + [0.0] * (groups - 1)
    for turn, ahead in sends(groups, chips):
        route = [
            (g * count + 2 * y + c, (g + turn) % groups * count + 2 * ((y + ahead) % chips) + c)
            for g in range(groups)
            for y in range(chips)
            for c in range(2)
        ]
        sent = lax.ppermute(rows_for(turn, ahead).astype(WIRE), ("grp", "seq"), route)
        received[turn] = received[turn] + sent.astype(F32)
    slots = []
    for slot in range(groups):
        piece = received[0]
        for turn in range(1, groups):
            piece = jnp.where((grp - slot) % groups == turn, received[turn], piece)
        slots.append(piece)
    return jnp.stack(slots, 1).reshape(queries.shape[0], lines, feats)


def sends(groups, chips):
    across = [(turn, ahead) for ahead in range(1, chips) for turn in reversed(range(groups))]
    beside = [(turn, 0) for turn in range(1, groups)]
    return beside + across


def solution(mesh):
    return jax.shard_map(
        per_device,
        mesh=mesh,
        in_specs=(
            P("head", "seq", None),
            P("head", "seq", None),
            P("head", "seq", None),
            P("head", None, None),
        ),
        out_specs=P("head", ("grp", "seq"), None),
        check_vma=False,
    )
```

```python
import jax
import jax.numpy as jnp
from jax import lax
from jax.experimental import pallas as pl
from jax.experimental.pallas import tpu as pltpu
from jax.sharding import PartitionSpec as P

F32 = jnp.float32
BF16 = jnp.bfloat16
WIRE = BF16
NN = (((1,), (0,)), ((), ()))
NT = (((1,), (1,)), ((), ()))
TN = (((0,), (0,)), ((), ()))


def mm(a, b, dims=NN):
    return lax.dot_general(a, b, dims, preferred_element_type=F32)


def split(x):
    high = x.astype(BF16)
    return high, (x - high.astype(F32)).astype(BF16)


def cat(parts, axis):
    return jnp.concatenate(parts, axis)


def interleave(make, heads, step):
    def group(i, _):
        running = [make(i * step + j) for j in range(step)]
        while running:
            running = [r for r in running if next(r, True) is None]
        return 0

    lax.fori_loop(0, heads // step, group, 0)


def add_rows(x):
    return jnp.sum(x, axis=0, keepdims=True)


def own_block(core, kv_own, kv_pair):
    tokens = kv_own.shape[1]
    rows = 2 * tokens

    def position(axis):
        index = lax.broadcasted_iota(jnp.int32, (rows, rows), axis)
        return jnp.where((index < tokens) == (core == 0), index % tokens, tokens + index % tokens)

    key = cat([kv_own[0], kv_pair[0]], 0)
    value = cat([kv_own[1], kv_pair[1]], 0)
    return position(0) <= position(1), key, value


def features(wmat_t, query, key):
    return jnp.exp(mm(wmat_t, query, NT)), jnp.exp(mm(wmat_t, key, NT))


def first_body(step, place, q_own, q_pair, w_ref, kv_own, kv_pair, state_ref):
    dh = q_own.shape[-1]
    scale = 1.0 / (dh**0.5)
    seen, key, value = own_block(place[0], kv_own, kv_pair)
    value_t = value.T
    heads, _, _ = w_ref.shape

    def forward(h):
        query = cat([q_own[h], q_pair[h]], 0)
        wmat_t = w_ref[h].T
        phi_q, phi_k = features(wmat_t, query, key)
        yield
        p = jnp.where(seen, jnp.exp(mm(key, query, NT) * scale), 0.0)
        yield
        a = jnp.where(seen, mm(phi_k.astype(BF16), phi_q.astype(BF16), TN), 0.0)
        yield
        sums = cat([add_rows(p), add_rows(a), jnp.zeros((6, p.shape[1]), F32)], 0)
        state_ref[h, 2 * dh :] = sums
        state_ref[h, :dh] = mm(value_t, p.astype(BF16))
        yield
        state_ref[h, dh : 2 * dh] = mm(cat([value_t, value_t], 1), cat(split(a), 0))

    interleave(forward, heads, step)


def second_body(total, step, place, q_own, q_pair, w_ref, kv_own, kv_pair, state_ref, hop_own, hop_pair, grad_ref):
    dh = q_own.shape[-1]
    core, chip = place[0], place[1]
    scale = 1.0 / (dh**0.5)
    hops = hop_own.shape[0]
    heads, _, feats = w_ref.shape

    def hop_block(hop):
        key_j = cat([hop_own[hop, 0], hop_pair[hop, 0]], 0)
        return key_j, cat([hop_own[hop, 1], hop_pair[hop, 1]], 0)

    def cotangents(numer_t, denom_t, numer_s, denom_s):
        target = (numer_t * (1.0 / denom_t)).astype(BF16).astype(F32)
        inverse = 1.0 / denom_s
        student = numer_s * inverse
        g = ((student - target) * (inverse * (2.0 / total))).astype(BF16)
        return g, add_rows(g.astype(F32) * student)

    def score_back(seen, value, g, shift):
        return split(jnp.where(seen, mm(value, g) - shift, 0.0))

    def local_back(dah, dal, qh, kh):
        dphi_q = mm(cat([kh, kh], 1), cat([dah, dal], 0))
        return dphi_q, mm(cat([qh, qh], 1), cat([dah, dal], 1), NT)

    def stacked(dz):
        return cat(split(dz), 0)

    def saved(h):
        numer_t, numer_s = state_ref[h, :dh], state_ref[h, dh : 2 * dh]
        sums = state_ref[h, 2 * dh :]
        return numer_t, sums[0:1], numer_s, sums[1:2]

    def finish(h, wide):
        grad_ref[h] = (wide[:feats] + wide[feats:]).T

    def whole(h):
        seen, key, value = own_block(core, kv_own, kv_pair)
        query = cat([q_own[h], q_pair[h]], 0)
        wmat_t = w_ref[h].T

        def earlier(hop, carry):
            state, state_t, total_j, numer_t, denom_t = carry[:5]
            key_j, value_j = hop_block(hop)
            if pre is None:
                p = jnp.exp(mm(key_j, query, NT) * scale)
                phi_j = jnp.exp(mm(wmat_t, key_j, NT))
            else:
                p, phi_j = pre
            ph = phi_j.astype(BF16)
            value_jt = value_j.T
            denom_t = denom_t + add_rows(p)
            numer_t = numer_t + mm(value_jt, p.astype(BF16))
            state = state + mm(ph, value_j)
            state_t = state_t + mm(value_jt, ph, NT)
            total_j = total_j + jnp.sum(ph.astype(F32), axis=1, keepdims=True)
            sums = (state, state_t, total_j, numer_t, denom_t)
            return sums + (phi_j,) if hops == 1 else sums

        numer_t, denom_t, numer_s, denom_s = saved(h)
        phi_q, phi_k = features(wmat_t, query, key)
        qh, kh = phi_q.astype(BF16), phi_k.astype(BF16)
        square = jnp.zeros((feats, dh), F32), jnp.zeros((dh, feats), F32)
        carry = square + (jnp.zeros((feats, 1), F32), numer_t, denom_t)
        pre = None
        if hops == 1:
            key_j = hop_block(0)[0]
            phi_j = jnp.exp(mm(wmat_t, key_j, NT))
            yield
            pre = jnp.exp(mm(key_j, query, NT) * scale), phi_j
            yield
            carry = earlier(0, carry)
        else:
            carry = lax.fori_loop(0, chip, earlier, carry)
        state, state_t, total_j, numer_t, denom_t = carry[:5]
        yield
        numer_s = numer_s + mm(cat(split(state_t), 1), cat([qh, qh], 0))
        denom_s = denom_s + add_rows(qh.astype(F32) * total_j)
        yield
        g, shift = cotangents(numer_t, denom_t, numer_s, denom_s)
        yield
        dah, dal = score_back(seen, value, g, shift)
        ds = mm(qh, g, NT)
        yield
        dphi_q, dphi_k = local_back(dah, dal, qh, kh)
        yield
        lost = jnp.sum(qh.astype(F32) * shift, axis=1, keepdims=True)
        dphi_q = dphi_q + mm(cat(split(state), 1), cat([g, g], 0)) - total_j * shift
        yield
        dsw = cat(split(ds), 1)

        def step_back(value_j, phi_j):
            return stacked((mm(dsw, cat([value_j, value_j], 1), NT) - lost) * phi_j)

        if hops == 1:
            key_j, value_j = hop_block(0)
            dz_j = step_back(value_j, carry[5])
            yield
            dz_q = stacked(dphi_q * phi_q)
            dz_k = stacked(dphi_k * phi_k)
            yield
            wide = mm(cat([dz_q, dz_k, dz_j], 1), cat([query, key, key_j], 0))
        else:
            dz = cat([stacked(dphi_q * phi_q), stacked(dphi_k * phi_k)], 1)
            wide = mm(dz, cat([query, key], 0))

            def back(hop, wide):
                key_j, value_j = hop_block(hop)
                phi_j = jnp.exp(mm(wmat_t, key_j, NT))
                return wide + mm(step_back(value_j, phi_j), key_j)

            wide = lax.fori_loop(0, chip, back, wide)
        yield
        finish(h, wide)

    @pl.when(chip != 0)
    def _():
        interleave(whole, heads, step)

    def alone(h):
        seen, key, value = own_block(core, kv_own, kv_pair)
        query = cat([q_own[h], q_pair[h]], 0)
        wmat_t = w_ref[h].T
        numer_t, denom_t, numer_s, denom_s = saved(h)
        phi_q, phi_k = features(wmat_t, query, key)
        qh, kh = phi_q.astype(BF16), phi_k.astype(BF16)
        g, shift = cotangents(numer_t, denom_t, numer_s, denom_s)
        yield
        dah, dal = score_back(seen, value, g, shift)
        yield
        dphi_q, dphi_k = local_back(dah, dal, qh, kh)
        yield
        dz = cat([stacked(dphi_q * phi_q), stacked(dphi_k * phi_k)], 1)
        wide = mm(dz, cat([query, key], 0))
        yield
        finish(h, wide)

    @pl.when(chip == 0)
    def _():
        interleave(alone, heads, step)


def call(function, outs, *operands):
    vmem = pl.BlockSpec(memory_space=pltpu.VMEM)
    return pl.pallas_call(
        function,
        in_specs=[pl.BlockSpec(memory_space=pltpu.SMEM)] + [vmem] * (len(operands) - 1),
        out_specs=[vmem] * len(outs),
        out_shape=[jax.ShapeDtypeStruct(s, F32) for s in outs],
        compiler_params=pltpu.CompilerParams(vmem_limit_bytes=16 << 20),
        cost_estimate=pl.CostEstimate(flops=2 * 10**9, bytes_accessed=10**7, transcendentals=10**6),
    )(*operands)


def per_device(queries, keys, values, feature_map):
    count, groups = lax.axis_size("seq"), lax.axis_size("grp")
    chips = count // 2
    seq, grp = lax.axis_index("seq"), lax.axis_index("grp")
    core, chip = seq & 1, seq >> 1
    tokens, dh = keys.shape[1:]
    total = tokens * count
    feats = feature_map.shape[2]
    hn = queries.shape[0] // (2 * groups)
    lines = dh // (groups * count)
    step = hn if hn <= 4 else 1
    swap = [(i, i ^ 1) for i in range(count)]

    def mine(array, half):
        split_heads = array.reshape(2 * groups, hn, *array.shape[1:])
        return lax.dynamic_index_in_dim(split_heads, half * groups + grp, 0, False)

    kv = jnp.where(lax.broadcasted_iota(jnp.int32, (2, tokens, dh), 0) == 0, keys, values)
    hops = []
    for k in range(1, chips):
        ring = [(i, (i + 2 * k) % count ^ 1) for i in range(count)]
        hops.append(lax.ppermute(kv, "seq", ring))
    place = jnp.stack([core, chip]).astype(jnp.int32)
    kv_pair = lax.ppermute(kv, "seq", swap)
    q_pair = lax.ppermute(mine(queries, 1 - core), "seq", swap)
    local = (place, mine(queries, core), q_pair, mine(feature_map, core), kv, kv_pair)
    rows = 2 * tokens
    state = [(hn, 2 * dh + 8, rows)]
    state = call(lambda *r: first_body(step, *r), state, *local)
    hop_own = jnp.stack(hops)
    hop_pair = lax.ppermute(hop_own, "seq", swap)
    (grad,) = call(
        lambda *r: second_body(total, step, *r),
        [(hn, dh, feats)],
        *local,
        *state,
        hop_own,
        hop_pair,
    )
    grad = grad.reshape(hn, groups, chips, 2, lines, feats)
    chip_of = lax.broadcasted_iota(jnp.int32, (1, groups, chips, 1, 1), 2)
    here = (lax.broadcasted_iota(jnp.int32, chip_of.shape, 1) == grp) & (chip_of == chip)
    straight = lax.dynamic_index_in_dim(grad, core, 3, False)
    crossed = lax.dynamic_index_in_dim(grad, 1 - core, 3, False)
    keep = jnp.where(here, straight, crossed)
    got = lax.ppermute(jnp.where(here, crossed, straight), "seq", swap)
    low = core == 0
    part = jnp.stack([jnp.where(low, keep, got), jnp.where(low, got, keep)])

    def rows_for(turn, ahead):
        there = lax.dynamic_index_in_dim(part, (grp + turn) % groups, 2, False)
        return lax.dynamic_index_in_dim(there, (chip + ahead) % chips, 2, False)

    received = [rows_for(0, 0)] + [0.0] * (groups - 1)
    for turn, ahead in sends(groups, chips):
        route = [
            (g * count + 2 * y + c, (g + turn) % groups * count + 2 * ((y + ahead) % chips) + 1 - c)
            for g in range(groups)
            for y in range(chips)
            for c in range(2)
        ]
        sent = lax.ppermute(rows_for(turn, ahead).astype(WIRE), ("grp", "seq"), route)
        received[turn] = received[turn] + sent.astype(F32)
    slots = []
    for slot in range(groups):
        piece = received[0]
        for turn in range(1, groups):
            piece = jnp.where((grp - slot) % groups == turn, received[turn], piece)
        slots.append(piece)
    return jnp.stack(slots, 1).reshape(queries.shape[0], lines, feats)


def sends(groups, chips):
    across = [(turn, ahead) for ahead in range(1, chips) for turn in reversed(range(groups))]
    beside = [(turn, 0) for turn in range(1, groups)]
    return beside + across


def solution(mesh):
    return jax.shard_map(
        per_device,
        mesh=mesh,
        in_specs=(
            P("head", "seq", None),
            P("head", "seq", None),
            P("head", "seq", None),
            P("head", None, None),
        ),
        out_specs=P("head", ("grp", "seq"), None),
        check_vma=False,
    )
```

```python
import jax
import jax.numpy as jnp
from jax import lax
from jax.experimental import pallas as pl
from jax.experimental.pallas import tpu as pltpu
from jax.sharding import PartitionSpec as P

F32 = jnp.float32
BF16 = jnp.bfloat16
WIRE = BF16
NN = (((1,), (0,)), ((), ()))
NT = (((1,), (1,)), ((), ()))
TN = (((0,), (0,)), ((), ()))


def mm(a, b, dims=NN):
    return lax.dot_general(a, b, dims, preferred_element_type=F32)


def split(x):
    high = x.astype(BF16)
    return high, (x - high.astype(F32)).astype(BF16)


def cat(parts, axis):
    return jnp.concatenate(parts, axis)


def interleave(make, heads, step):
    def group(i, _):
        running = [make(i * step + j) for j in range(step)]
        while running:
            running = [r for r in running if next(r, True) is None]
        return 0

    lax.fori_loop(0, heads // step, group, 0)


def add_rows(x):
    return jnp.sum(x, axis=0, keepdims=True)


def own_block(core, kv_own, kv_pair):
    tokens = kv_own.shape[1]
    rows = 2 * tokens

    def position(axis):
        index = lax.broadcasted_iota(jnp.int32, (rows, rows), axis)
        return jnp.where((index < tokens) == (core == 0), index % tokens, tokens + index % tokens)

    key = cat([kv_own[0], kv_pair[0]], 0)
    value = cat([kv_own[1], kv_pair[1]], 0)
    return position(0) <= position(1), key, value


def features(wmat_t, query, key):
    return jnp.exp(mm(wmat_t, query, NT)), jnp.exp(mm(wmat_t, key, NT))


def first_body(step, place, q_own, q_pair, w_ref, kv_own, kv_pair, state_ref):
    dh = q_own.shape[-1]
    scale = 1.0 / (dh**0.5)
    seen, key, value = own_block(place[0], kv_own, kv_pair)
    value_t = value.T
    heads, _, _ = w_ref.shape

    def forward(h):
        query = cat([q_own[h], q_pair[h]], 0)
        wmat_t = w_ref[h].T
        phi_q, phi_k = features(wmat_t, query, key)
        yield
        p = jnp.where(seen, jnp.exp(mm(key, query, NT) * scale), 0.0)
        yield
        a = jnp.where(seen, mm(phi_k.astype(BF16), phi_q.astype(BF16), TN), 0.0)
        yield
        sums = cat([add_rows(p), add_rows(a), jnp.zeros((6, p.shape[1]), F32)], 0)
        state_ref[h, 2 * dh :] = sums
        state_ref[h, :dh] = mm(value_t, p.astype(BF16))
        yield
        state_ref[h, dh : 2 * dh] = mm(cat([value_t, value_t], 1), cat(split(a), 0))

    interleave(forward, heads, step)


def second_body(total, step, place, q_own, q_pair, w_ref, kv_own, kv_pair, state_ref, hop_own, hop_pair, grad_ref):
    dh = q_own.shape[-1]
    core, chip = place[0], place[1]
    scale = 1.0 / (dh**0.5)
    hops = hop_own.shape[0]
    heads, _, feats = w_ref.shape

    def hop_block(hop):
        key_j = cat([hop_own[hop, 0], hop_pair[hop, 0]], 0)
        return key_j, cat([hop_own[hop, 1], hop_pair[hop, 1]], 0)

    def cotangents(numer_t, denom_t, numer_s, denom_s):
        target = (numer_t * (1.0 / denom_t)).astype(BF16).astype(F32)
        inverse = 1.0 / denom_s
        student = numer_s * inverse
        g = ((student - target) * (inverse * (2.0 / total))).astype(BF16)
        return g, add_rows(g.astype(F32) * student)

    def score_back(seen, value, g, shift):
        return split(jnp.where(seen, mm(value, g) - shift, 0.0))

    def local_back(dah, dal, qh, kh):
        dphi_q = mm(cat([kh, kh], 1), cat([dah, dal], 0))
        return dphi_q, mm(cat([qh, qh], 1), cat([dah, dal], 1), NT)

    def stacked(dz):
        return cat(split(dz), 0)

    def saved(h):
        numer_t, numer_s = state_ref[h, :dh], state_ref[h, dh : 2 * dh]
        sums = state_ref[h, 2 * dh :]
        return numer_t, sums[0:1], numer_s, sums[1:2]

    def finish(h, wide):
        grad_ref[h] = (wide[:feats] + wide[feats:]).T

    def whole(h):
        seen, key, value = own_block(core, kv_own, kv_pair)
        query = cat([q_own[h], q_pair[h]], 0)
        wmat_t = w_ref[h].T

        def earlier(hop, carry):
            state, state_t, total_j, numer_t, denom_t = carry[:5]
            key_j, value_j = hop_block(hop)
            if pre is None:
                p = jnp.exp(mm(key_j, query, NT) * scale)
                phi_j = jnp.exp(mm(wmat_t, key_j, NT))
            else:
                p, phi_j = pre
            ph = phi_j.astype(BF16)
            value_jt = value_j.T
            denom_t = denom_t + add_rows(p)
            numer_t = numer_t + mm(value_jt, p.astype(BF16))
            state = state + mm(ph, value_j)
            state_t = state_t + mm(value_jt, ph, NT)
            total_j = total_j + jnp.sum(ph.astype(F32), axis=1, keepdims=True)
            sums = (state, state_t, total_j, numer_t, denom_t)
            return sums + (phi_j,) if hops == 1 else sums

        numer_t, denom_t, numer_s, denom_s = saved(h)
        phi_q, phi_k = features(wmat_t, query, key)
        qh, kh = phi_q.astype(BF16), phi_k.astype(BF16)
        square = jnp.zeros((feats, dh), F32), jnp.zeros((dh, feats), F32)
        carry = square + (jnp.zeros((feats, 1), F32), numer_t, denom_t)
        pre = None
        if hops == 1:
            key_j = hop_block(0)[0]
            phi_j = jnp.exp(mm(wmat_t, key_j, NT))
            yield
            pre = jnp.exp(mm(key_j, query, NT) * scale), phi_j
            yield
            carry = earlier(0, carry)
        else:
            carry = lax.fori_loop(0, chip, earlier, carry)
        state, state_t, total_j, numer_t, denom_t = carry[:5]
        yield
        numer_s = numer_s + mm(cat(split(state_t), 1), cat([qh, qh], 0))
        denom_s = denom_s + add_rows(qh.astype(F32) * total_j)
        yield
        g, shift = cotangents(numer_t, denom_t, numer_s, denom_s)
        yield
        dah, dal = score_back(seen, value, g, shift)
        ds = mm(qh, g, NT)
        yield
        dphi_q, dphi_k = local_back(dah, dal, qh, kh)
        yield
        lost = jnp.sum(qh.astype(F32) * shift, axis=1, keepdims=True)
        dphi_q = dphi_q + mm(cat(split(state), 1), cat([g, g], 0)) - total_j * shift
        yield
        dsw = cat(split(ds), 1)

        def step_back(value_j, phi_j):
            return stacked((mm(dsw, cat([value_j, value_j], 1), NT) - lost) * phi_j)

        if hops == 1:
            key_j, value_j = hop_block(0)
            dz_j = step_back(value_j, carry[5])
            yield
            dz_q = stacked(dphi_q * phi_q)
            dz_k = stacked(dphi_k * phi_k)
            yield
            wide = mm(cat([dz_q, dz_k, dz_j], 1), cat([query, key, key_j], 0))
        else:
            dz = cat([stacked(dphi_q * phi_q), stacked(dphi_k * phi_k)], 1)
            wide = mm(dz, cat([query, key], 0))

            def back(hop, wide):
                key_j, value_j = hop_block(hop)
                phi_j = jnp.exp(mm(wmat_t, key_j, NT))
                return wide + mm(step_back(value_j, phi_j), key_j)

            wide = lax.fori_loop(0, chip, back, wide)
        yield
        finish(h, wide)

    @pl.when(chip != 0)
    def _():
        interleave(whole, heads, step)

    def alone(h):
        seen, key, value = own_block(core, kv_own, kv_pair)
        query = cat([q_own[h], q_pair[h]], 0)
        wmat_t = w_ref[h].T
        numer_t, denom_t, numer_s, denom_s = saved(h)
        phi_q, phi_k = features(wmat_t, query, key)
        qh, kh = phi_q.astype(BF16), phi_k.astype(BF16)
        g, shift = cotangents(numer_t, denom_t, numer_s, denom_s)
        yield
        dah, dal = score_back(seen, value, g, shift)
        yield
        dphi_q, dphi_k = local_back(dah, dal, qh, kh)
        yield
        dz = cat([stacked(dphi_q * phi_q), stacked(dphi_k * phi_k)], 1)
        wide = mm(dz, cat([query, key], 0))
        yield
        finish(h, wide)

    @pl.when(chip == 0)
    def _():
        interleave(alone, heads, step)


def call(function, outs, *operands):
    vmem = pl.BlockSpec(memory_space=pltpu.VMEM)
    return pl.pallas_call(
        function,
        in_specs=[pl.BlockSpec(memory_space=pltpu.SMEM)] + [vmem] * (len(operands) - 1),
        out_specs=[vmem] * len(outs),
        out_shape=[jax.ShapeDtypeStruct(s, F32) for s in outs],
        compiler_params=pltpu.CompilerParams(vmem_limit_bytes=16 << 20),
        cost_estimate=pl.CostEstimate(flops=2 * 10**9, bytes_accessed=10**7, transcendentals=10**6),
    )(*operands)


def per_device(queries, keys, values, feature_map):
    count, groups = lax.axis_size("seq"), lax.axis_size("grp")
    chips = count // 2
    seq, grp = lax.axis_index("seq"), lax.axis_index("grp")
    core, chip = seq & 1, seq >> 1
    tokens, dh = keys.shape[1:]
    total = tokens * count
    feats = feature_map.shape[2]
    hn = queries.shape[0] // (2 * groups)
    lines = dh // (groups * count)
    step = hn if hn <= 4 else 1
    swap = [(i, i ^ 1) for i in range(count)]

    def mine(array, half):
        split_heads = array.reshape(2 * groups, hn, *array.shape[1:])
        return lax.dynamic_index_in_dim(split_heads, half * groups + grp, 0, False)

    kv = jnp.where(lax.broadcasted_iota(jnp.int32, (2, tokens, dh), 0) == 0, keys, values)
    hops = []
    for k in range(1, chips):
        ring = [(i, (i + 2 * k) % count ^ 1) for i in range(count)]
        hops.append(lax.ppermute(kv, "seq", ring))
    place = jnp.stack([core, chip]).astype(jnp.int32)
    kv_pair = lax.ppermute(kv, "seq", swap)
    q_pair = lax.ppermute(mine(queries, 1 - core), "seq", swap)
    local = (place, mine(queries, core), q_pair, mine(feature_map, core), kv, kv_pair)
    rows = 2 * tokens
    state = [(hn, 2 * dh + 8, rows)]
    state = call(lambda *r: first_body(step, *r), state, *local)
    hop_own = jnp.stack(hops)
    hop_pair = lax.ppermute(hop_own, "seq", swap)
    (grad,) = call(
        lambda *r: second_body(total, step, *r),
        [(hn, dh, feats)],
        *local,
        *state,
        hop_own,
        hop_pair,
    )
    grad = grad.reshape(hn, groups, chips, 2, lines, feats)
    chip_of = lax.broadcasted_iota(jnp.int32, (1, groups, chips, 1, 1), 2)
    here = (lax.broadcasted_iota(jnp.int32, chip_of.shape, 1) == grp) & (chip_of == chip)
    straight = lax.dynamic_index_in_dim(grad, core, 3, False)
    crossed = lax.dynamic_index_in_dim(grad, 1 - core, 3, False)
    keep = jnp.where(here, straight, crossed)
    got = lax.ppermute(jnp.where(here, crossed, straight).astype(WIRE), "seq", swap)
    got = got.astype(F32)
    low = core == 0
    part = jnp.stack([jnp.where(low, keep, got), jnp.where(low, got, keep)])

    def rows_for(turn, ahead):
        there = lax.dynamic_index_in_dim(part, (grp + turn) % groups, 2, False)
        return lax.dynamic_index_in_dim(there, (chip + ahead) % chips, 2, False)

    received = [rows_for(0, 0)] + [0.0] * (groups - 1)
    for turn, ahead in sends(groups, chips):
        route = [
            (g * count + 2 * y + c, (g + turn) % groups * count + 2 * ((y + ahead) % chips) + 1 - c)
            for g in range(groups)
            for y in range(chips)
            for c in range(2)
        ]
        sent = lax.ppermute(rows_for(turn, ahead).astype(WIRE), ("grp", "seq"), route)
        received[turn] = received[turn] + sent.astype(F32)
    slots = []
    for slot in range(groups):
        piece = received[0]
        for turn in range(1, groups):
            piece = jnp.where((grp - slot) % groups == turn, received[turn], piece)
        slots.append(piece)
    return jnp.stack(slots, 1).reshape(queries.shape[0], lines, feats)


def sends(groups, chips):
    across = [(turn, ahead) for ahead in range(1, chips) for turn in reversed(range(groups))]
    beside = [(turn, 0) for turn in range(1, groups)]
    return across[:1] + beside + across[1:]


def solution(mesh):
    return jax.shard_map(
        per_device,
        mesh=mesh,
        in_specs=(
            P("head", "seq", None),
            P("head", "seq", None),
            P("head", "seq", None),
            P("head", None, None),
        ),
        out_specs=P("head", ("grp", "seq"), None),
        check_vma=False,
    )
```
